512 devices in a mesh: fsdp: 32 (over z, y_lo, core), dp: 4 (over y_hi), tensor: 4 (over x).
Axes of the slice: x: 4, y: 8 (y_hi: 4, y_lo: 2; y = y_hi * 2 + y_lo), z: 8, core: 2. Of those that a mesh axis runs over, the one named last changes fastest.
Arguments:
- master_weight: float32 [4096, 14336], P(('fsdp', 'dp'), 'tensor'), may hold values from -0.09375 to 0.09375
- first_moment: bfloat16 [4096, 14336], P(('fsdp', 'dp'), 'tensor'), may hold values from -6 to 6
- second_moment: bfloat16 [4096, 14336], P(('fsdp', 'dp'), 'tensor'), may hold values from 0.25 to 16
- teacher_weight: float32 [4096, 14336], P(('fsdp', 'dp'), 'tensor'), may hold values from -0.09375 to 0.09375
- grad_parts: bfloat16 [4, 4096, 14336], P('dp', 'fsdp', 'tensor'), may hold values from -6 to 6
- embed_table: bfloat16 [4096, 64128], P(('fsdp', 'dp', 'tensor')), may hold values from -6 to 6
- token_ids: int32 [32, 256], P('fsdp'), may hold values from 0 to 64127
- pair_ids: int32 [32, 256], P('fsdp'), may hold values from 0 to 7, never falling along the last dimension, each value on 1 to 64 neighbouring positions
- class_head: bfloat16 [4, 3584, 256], P('tensor', 'dp'), may hold values from -0.046875 to 0.046875
Outputs:
- master_new: float32 [4096, 14336], P(('fsdp', 'dp'), 'tensor')
- first_new: bfloat16 [4096, 14336], P(('fsdp', 'dp'), 'tensor')
- second_new: bfloat16 [4096, 14336], P(('fsdp', 'dp'), 'tensor')
- teacher_new: float32 [4096, 14336], P(('fsdp', 'dp'), 'tensor')
- class_logits: float32 [32, 8, 256], P('fsdp')
The draws below stay inside these ranges and needn't reach their ends.
Inputs may be any that keep to these rules, and one draw needn't show every extreme that they name: `pair_ids`: in every row the pair numbers never fall, and each of the 8 pairs holds 1 to 64 tokens, one of them exactly 64.
All inputs are finite; a program needn't handle non-finite values.
Results may differ from the reference program's by a relative error of at most 0.0055.
Values may be sent and summed in bfloat16 or wider, within the bound.
No kernel may reach another device: no remote copies, remote signals or barrier semaphores. Data moves between devices by JAX's collectives and lax.ppermute only.
A program may use at most 128 MiB of HBM per device.

```python
import math
import jax
import jax.numpy as jnp
import numpy as np
from jax import lax

D = 4096
FF = 14336
VOCAB = 64128
CLASSES = 256
PAIRS = 8
TOK_GRP = 256
MOST = 64
FF_T = 3584
N_FSDP = 32
N_DP = 4
N_TENSOR = 4


def draw_embed_table(key, part):
    key_rows, key_cols, key_base = jax.random.split(key, 3)
    row_scale = jnp.exp(jax.random.uniform(key_rows, (D, 1), jnp.float32, 0.0, 2.5))
    col_scale = jnp.exp(jax.random.uniform(key_cols, (1, VOCAB), jnp.float32, 0.0, 2.5))
    base = jax.random.truncated_normal(key_base, -4.0, 4.0, (D, VOCAB), jnp.float32)
    return (0.01 * row_scale * col_scale * base).astype(jnp.bfloat16)


def touch_ends(result, rng, low, largest):
    place = [jax.random.randint(jax.random.fold_in(rng, axis), (), 0, length) for axis, length in enumerate(result.shape)]
    widest = result.shape.index(max(result.shape))
    neighbour = place[:widest] + [(place[widest] + 1) % result.shape[widest]] + place[widest + 1:]
    return result.at[tuple(place)].set(low).at[tuple(neighbour)].set(largest)


def strengthened(drawn, rng, source, target, parts, factor):
    owner, partner = [(jnp.arange(drawn.shape[axis_at]) // (drawn.shape[axis_at] // parts)).reshape([-1 if axis == axis_at else 1 for axis in range(drawn.ndim)]) for axis_at in (source, target)]
    chosen = jax.random.permutation(rng, parts)[partner]
    strong = (owner == chosen) | (owner == (partner + parts // 2) % parts)
    return jnp.where(strong, factor * drawn, drawn)


def block_levels(rng, shape, cuts, smallest, top_value):
    def one(dim, parts):
        steps = jax.random.uniform(jax.random.fold_in(jax.random.fold_in(rng, 6), dim), (parts,), jnp.float32, smallest / len(cuts), top_value / len(cuts))
        return jnp.repeat(jnp.exp(steps), shape[dim] // parts).reshape((-1,) + (1,) * (len(shape) - dim - 1))

    level = one(*cuts[0])
    for cut in cuts[1:]:
        level = level * one(*cut)
    return level


def rank_table(amount, skew):
    weights = [(1 << 20) // math.isqrt(grade ** skew) + 1 for grade in range(1, amount + 1)]
    scale = 1 + sum(weights) // (1 << 30)
    return np.cumsum(np.array([max(1, weight // scale) for weight in weights]))


def ranked_ids(rng, dims, count, slope):
    listing = rank_table(count, slope)
    ticket = jax.random.randint(jax.random.fold_in(rng, 1), dims, 0, int(listing[count - 1]))
    standing = jnp.searchsorted(jnp.asarray(listing, jnp.int32), ticket, side="right")
    return jax.random.permutation(jax.random.fold_in(rng, 2), count)[standing].astype(jnp.int32)


def profile(number_of, total, limit, skew):
    weights = [(1 << 20) // math.isqrt(grade ** skew) + 1 for grade in range(2, number_of + 1)]
    surplus, counts = total - limit - (number_of - 1), [1] * (number_of - 1)
    while surplus > 0:
        free = [i for i in range(number_of - 1) if counts[i] < limit]
        pool, left = sum([weights[i] for i in free]), surplus
        for i in free:
            addition = min(limit - counts[i], max(1, left * weights[i] // pool), surplus)
            counts[i] = counts[i] + addition
            surplus = surplus - addition
    return np.array([limit] + counts)


def uneven_parts(stream_key, number_of, total, most, skew):
    if number_of == 2:
        one = jax.random.randint(stream_key, (), max(1, total - most), min(most, total - 1) + 1)
        return jnp.stack([one, total - one])
    tallies = jnp.asarray(profile(number_of, total, most, skew), jnp.int32)
    twos = (number_of - 1) // 2
    donor, receiver = tallies[1:1 + 2 * twos:2], tallies[2:2 + 2 * twos:2]
    slack = jnp.minimum(donor - 1, most - receiver)
    moved = jax.random.randint(jax.random.fold_in(stream_key, 1), (twos,), 0, 1 << 20) % (slack + 1)
    tallies = tallies.at[1:1 + 2 * twos:2].set(donor - moved).at[2:2 + 2 * twos:2].set(receiver + moved)
    return tallies[jax.random.permutation(jax.random.fold_in(stream_key, 2), number_of)]


def centred(stream_key, extent, deviation, most, cuts=(), kind=jnp.bfloat16):
    result = jax.random.normal(stream_key, extent, jnp.float32) * deviation
    if len(cuts) > 0:
        result = block_levels(stream_key, extent, cuts, -0.22, 0.18) * result
    return jnp.clip(result, min=-most, max=most).astype(kind)


def gaussian_with(rng, dims, scale, reach, cuts, heavy, kind=jnp.bfloat16):
    result = scale * jax.random.normal(rng, dims, jnp.float32)
    if cuts:
        result = result * block_levels(rng, dims, cuts, -0.22, 0.18)
    return jnp.clip(strengthened(result, jax.random.fold_in(rng, 3), *heavy), -reach, reach).astype(kind)


def setup_inputs(seed: int = 0) -> dict:
    key_of = jax.random.split(jax.random.key(seed), 10)
    master_weight = centred(key_of[0], (D, FF), D ** -0.5, 0.09375, ((0, 128), (1, 4)), jnp.float32)
    first_moment = centred(key_of[1], (D, FF), 1.0, 6.0, ((0, 128), (1, 4)))
    second_moment = jnp.clip(jnp.exp(math.log(16.0) - 4.158883 * jax.random.uniform(key_of[2], (D, FF), jnp.float32) ** block_levels(key_of[2], (D, FF), ((0, 128), (1, 4)), -0.2, 0.2)), 0.25, 16.0).astype(jnp.bfloat16)
    teacher_weight = centred(key_of[3], (D, FF), D ** -0.5, 0.09375, ((0, 128), (1, 4)), jnp.float32)
    grad_parts = gaussian_with(key_of[4], (N_DP, D, FF), 1.0, 6.0, ((0, 4), (1, 32), (2, 4)), (0, 1, 4, 2.0))
    embed_table = draw_embed_table(jax.random.fold_in(key_of[9], 71), 0)
    token_ids = touch_ends(ranked_ids(key_of[6], (N_FSDP, TOK_GRP), VOCAB, 2), jax.random.fold_in(key_of[6], 3), 0, VOCAB - 1).astype(jnp.int32)
    pair_ids = jax.vmap(lambda own: jnp.searchsorted(jnp.cumsum(uneven_parts(own, PAIRS, TOK_GRP, MOST, 1)), jnp.arange(TOK_GRP), side="right"))(jax.random.split(key_of[7], N_FSDP)).reshape((N_FSDP, TOK_GRP)).astype(jnp.int32)
    class_head = centred(key_of[8], (N_TENSOR, FF_T, CLASSES), FF ** -0.5, 0.046875, ((0, 4), (1, 4)))
    return {"master_weight": master_weight, "first_moment": first_moment, "second_moment": second_moment, "teacher_weight": teacher_weight, "grad_parts": grad_parts, "embed_table": embed_table, "token_ids": token_ids, "pair_ids": pair_ids, "class_head": class_head}


beta_one = 0.9
beta_two = 0.95
learn_rate = 0.001
decay_rate = 0.1
ema_keep = 0.99

def reference(master_weight, first_moment, second_moment, teacher_weight, grad_parts, embed_table, token_ids, pair_ids, class_head):
    gradient = grad_parts[0].astype(jnp.float32)
    for member in range(1, N_DP):
        gradient = gradient + grad_parts[member].astype(jnp.float32)
    first_full = beta_one * first_moment.astype(jnp.float32) + (1.0 - beta_one) * gradient
    second_full = beta_two * second_moment.astype(jnp.float32) + (1.0 - beta_two) * gradient * gradient
    master_new = master_weight - learn_rate * (first_full / (jnp.sqrt(second_full) + 1e-08) + decay_rate * master_weight)
    teacher_new = ema_keep * teacher_weight + (1.0 - ema_keep) * master_new
    teacher_half = teacher_new.astype(jnp.bfloat16)
    head_rows = class_head.reshape(FF, CLASSES)

    def label_group(inputs):
        group_ids, group_pairs = inputs
        picked = jnp.take(embed_table, group_ids, axis=1).astype(jnp.float32)
        scale = lax.rsqrt(lax.optimization_barrier(jnp.mean(picked * picked, axis=0, keepdims=True)) + 1e-05)
        normed = (picked * scale).astype(jnp.bfloat16)
        hidden = jnp.dot(normed.T, teacher_half, preferred_element_type=jnp.float32)
        active = jax.nn.silu(hidden)
        member_of = (group_pairs[None, :] == jnp.arange(PAIRS, dtype=jnp.int32)[:, None]).astype(jnp.float32)
        totals = jnp.dot(member_of, active, precision=lax.Precision.HIGHEST)
        pooled = (totals / lax.optimization_barrier(jnp.sum(member_of, axis=1, keepdims=True))).astype(jnp.bfloat16)
        return jnp.dot(pooled, head_rows, preferred_element_type=jnp.float32)
    class_logits = lax.map(label_group, (token_ids, pair_ids))
    return (master_new, first_full.astype(jnp.bfloat16), second_full.astype(jnp.bfloat16), teacher_new, class_logits)
```

```python
import jax
import jax.numpy as jnp
from jax import lax
from jax.sharding import PartitionSpec as P

PAIRS = 8


beta_one = 0.9
beta_two = 0.95
learn_rate = 0.001
decay_rate = 0.1
ema_keep = 0.99


def optimizer_step(master_weight, first_moment, second_moment, teacher_weight, grad_parts):
    gradient = lax.psum_scatter(
        grad_parts[0], "dp", scatter_dimension=0, tiled=True
    ).astype(jnp.float32)
    first_full = beta_one * first_moment.astype(jnp.float32) + (1.0 - beta_one) * gradient
    second_full = (
        beta_two * second_moment.astype(jnp.float32) + (1.0 - beta_two) * gradient * gradient
    )
    master_new = master_weight - learn_rate * (
        first_full / (jnp.sqrt(second_full) + 1e-08) + decay_rate * master_weight
    )
    teacher_new = ema_keep * teacher_weight + (1.0 - ema_keep) * master_new
    return (
        master_new,
        first_full.astype(jnp.bfloat16),
        second_full.astype(jnp.bfloat16),
        teacher_new,
    )


def ring_gather(block, axis):
    count = lax.axis_size(axis)
    right = [(i, (i + 1) % count) for i in range(count)]
    left = [(i, (i - 1) % count) for i in range(count)]
    place = lax.axis_index(axis)
    half = block.shape[0] // 2
    whole = jnp.zeros((count,) + block.shape, block.dtype)
    whole = lax.dynamic_update_index_in_dim(whole, block, place, 0)
    going_right = going_left = block
    for step in range(1, count // 2):
        going_right = lax.ppermute(going_right, axis, right)
        going_left = lax.ppermute(going_left, axis, left)
        whole = lax.dynamic_update_index_in_dim(whole, going_right, (place - step) % count, 0)
        whole = lax.dynamic_update_index_in_dim(whole, going_left, (place + step) % count, 0)
    first = lax.ppermute(going_right[:half], axis, right)
    second = lax.ppermute(going_left[half:], axis, left)
    last = jnp.concatenate([first, second], axis=0)
    return lax.dynamic_update_index_in_dim(whole, last, (place + count // 2) % count, 0)


def embed_inputs(embed_table, token_ids):
    every_id = lax.all_to_all(
        jnp.broadcast_to(token_ids, (32, token_ids.shape[1])), "fsdp", 0, 0, tiled=True
    )
    picked = embed_table.at[:, every_id.reshape(-1)].get(mode="promise_in_bounds")
    received = lax.all_to_all(
        picked.reshape(8, 32, 256).transpose(1, 0, 2), "fsdp", split_axis=0, concat_axis=0, tiled=True
    )
    part = lax.all_gather(received.reshape(256, 256), "dp", axis=0, tiled=True)
    return ring_gather(part, "tensor")


def label_tokens(teacher_new, stacked, group_pairs, class_head):
    teacher_half = teacher_new.astype(jnp.bfloat16)
    replica_count = lax.axis_size("dp")
    rows = teacher_half.shape[0]
    width = teacher_half.shape[1] // replica_count
    split = teacher_half.reshape(rows, replica_count, width).transpose(1, 0, 2)
    block = lax.all_to_all(split.reshape(-1, width), "dp", 0, 0, tiled=True)
    row_block = lax.all_gather(block, "fsdp", axis=0, tiled=True)
    inputs = stacked.reshape(4, 4, 32, 8, 256).transpose(2, 1, 0, 3, 4).reshape(4096, 256)
    values = inputs.astype(jnp.float32)
    scale = lax.rsqrt(jnp.mean(values * values, axis=0, keepdims=True) + 1e-05)
    normed = (values * scale).astype(jnp.bfloat16)
    hidden = jnp.einsum("fk,fo->ko", normed, row_block, preferred_element_type=jnp.float32)
    group_count = group_pairs.shape[0]
    active = jax.nn.silu(hidden).reshape(group_count, -1, width)
    member_of = (
        group_pairs[:, None, :] == jnp.arange(PAIRS, dtype=jnp.int32)[None, :, None]
    ).astype(jnp.float32)
    totals = jnp.einsum("gpt,gtk->gpk", member_of, active, precision=lax.Precision.HIGHEST)
    pooled = (totals / jnp.sum(member_of, axis=2, keepdims=True)).astype(jnp.bfloat16)
    head_part = class_head[0]
    partial_terms = jnp.einsum("gpk,kc->gpc", pooled, head_part, preferred_element_type=jnp.float32)
    return lax.psum(lax.psum(partial_terms, "dp"), "tensor")


def shards(
    master_weight,
    first_moment,
    second_moment,
    teacher_weight,
    grad_parts,
    embed_table,
    token_ids,
    pair_ids,
    class_head,
):
    master_new, first_new, second_new, teacher_new = optimizer_step(
        master_weight, first_moment, second_moment, teacher_weight, grad_parts
    )
    stacked = embed_inputs(embed_table, token_ids)
    class_logits = label_tokens(teacher_new, stacked, pair_ids, class_head)
    return (master_new, first_new, second_new, teacher_new, class_logits)


def solution(mesh):
    placed = (
        P(("fsdp", "dp"), "tensor"),
        P(("fsdp", "dp"), "tensor"),
        P(("fsdp", "dp"), "tensor"),
        P(("fsdp", "dp"), "tensor"),
        P("dp", "fsdp", "tensor"),
        P(("fsdp", "dp", "tensor"), None),
        P("fsdp", None),
        P("fsdp", None),
        P("tensor", "dp", None),
    )
    return jax.shard_map(
        shards,
        mesh=mesh,
        in_specs=placed,
        out_specs=(
            P(("fsdp", "dp"), "tensor"),
            P(("fsdp", "dp"), "tensor"),
            P(("fsdp", "dp"), "tensor"),
            P(("fsdp", "dp"), "tensor"),
            P("fsdp", None, None),
        ),
        check_vma=False,
    )
```

```python
import functools

import jax
import jax.numpy as jnp
from jax import lax
from jax.experimental import pallas as pl
from jax.experimental.pallas import tpu as pltpu
from jax.sharding import Mesh
from jax.sharding import PartitionSpec as P

PAIRS = 8
TOKENS = 256
WIDTH = 896
UPPER = 512

beta_one = 0.9
beta_two = 0.95
learn_rate = 0.001
decay_rate = 0.1
ema_keep = 0.99

f32 = jnp.float32
bf16 = jnp.bfloat16
VMEM = pltpu.VMEM


def optimizer_kernel(
    place_ref, master_ref, first_ref, second_ref, teacher_ref, parts_ref,
    master_out, first_out, second_out, teacher_out, columns_out,
):
    gradient = parts_ref[0].astype(f32)
    for member in range(1, 4):
        gradient = gradient + parts_ref[member].astype(f32)
    first_full = beta_one * first_ref[...].astype(f32) + (1.0 - beta_one) * gradient
    second_full = (
        beta_two * second_ref[...].astype(f32) + (1.0 - beta_two) * gradient * gradient
    )
    master = master_ref[...]
    master_new = master - learn_rate * (
        first_full / (jnp.sqrt(second_full) + 1e-08) + decay_rate * master
    )
    teacher_new = ema_keep * teacher_ref[...] + (1.0 - ema_keep) * master_new
    master_out[...] = master_new
    first_out[...] = first_full.astype(bf16)
    second_out[...] = second_full.astype(bf16)
    teacher_out[...] = teacher_new
    columns_out[0] = teacher_new.astype(bf16)


def optimizer_step(place, master_weight, first_moment, second_moment, teacher_weight, parts):
    block = pl.BlockSpec((32, WIDTH), lambda k, place: (0, (place[0] + k) % 4))
    shape = master_weight.shape
    return pl.pallas_call(
        optimizer_kernel,
        grid_spec=pltpu.PrefetchScalarGridSpec(
            num_scalar_prefetch=1,
            grid=(4,),
            in_specs=[block] * 4
            + [pl.BlockSpec((4, 32, WIDTH), lambda k, place: (0, 0, (place[0] + k) % 4))],
            out_specs=[block] * 4 + [pl.BlockSpec((1, 32, WIDTH), lambda k, place: (k, 0, 0))],
        ),
        out_shape=[
            jax.ShapeDtypeStruct(shape, f32),
            jax.ShapeDtypeStruct(shape, bf16),
            jax.ShapeDtypeStruct(shape, bf16),
            jax.ShapeDtypeStruct(shape, f32),
            jax.ShapeDtypeStruct((4, 32, WIDTH), bf16),
        ],
        cost_estimate=pl.CostEstimate(flops=1 << 21, bytes_accessed=1 << 23, transcendentals=0),
        name="optimizer_step",
    )(place, master_weight, first_moment, second_moment, teacher_weight, parts)


def turn_table_kernel(table_ref, out_ref, wide, turned):
    count = table_ref.shape[0]
    wide[pl.ds(0, count)] = table_ref[...].astype(f32)
    wide[pl.ds(count, UPPER - count)] = jnp.zeros((UPPER - count, 8, 128), f32)
    for part in range(UPPER // 128):
        for row in range(8):
            turned[:, row, pl.ds(part * 128, 128)] = wide[pl.ds(part * 128, 128), row, :].T
    out_ref[...] = turned[...].reshape(1024, UPPER).astype(bf16)


def turn_table(table):
    tiles = table.reshape(8, -1, 128).transpose(1, 0, 2)
    return pl.pallas_call(
        turn_table_kernel,
        out_shape=jax.ShapeDtypeStruct((1024, UPPER), bf16),
        in_specs=[pl.BlockSpec(memory_space=VMEM)],
        out_specs=pl.BlockSpec(memory_space=VMEM),
        scratch_shapes=[VMEM((UPPER, 8, 128), f32), VMEM((128, 8, UPPER), f32)],
        cost_estimate=pl.CostEstimate(flops=0, bytes_accessed=1 << 24, transcendentals=0),
        name="turn_table",
    )(tiles)


def pick_kernel(ids_ref, table_ref, out_ref):
    ids = ids_ref[0]
    count = ids.shape[1]
    upper = ids >> 7
    lower = jnp.broadcast_to(ids & 127, (8, count))
    rows = lax.broadcasted_iota(jnp.int32, (UPPER, count), 0)
    hot = jnp.where(rows == upper, 1.0, 0.0).astype(bf16)
    picked = jnp.zeros((8, count), f32)
    for part in range(4):
        lines = jnp.dot(table_ref[pl.ds(part * 256, 256), :], hot, preferred_element_type=f32)
        for k in range(32):
            picked = jnp.where(lower == part * 32 + k, lines[k * 8 : (k + 1) * 8, :], picked)
    for copy in range(out_ref.shape[1]):
        out_ref[0, copy] = picked.astype(bf16)


def pick_tokens(ids, table):
    chips, _, count = ids.shape
    return pl.pallas_call(
        pick_kernel,
        grid=(chips,),
        in_specs=[
            pl.BlockSpec((1, 1, count), lambda i: (i, 0, 0)),
            pl.BlockSpec((1024, UPPER), lambda i: (0, 0)),
        ],
        out_specs=pl.BlockSpec((1, 4, 8, count), lambda i: (i, 0, 0, 0)),
        out_shape=jax.ShapeDtypeStruct((chips, 4, 8, count), bf16),
        cost_estimate=pl.CostEstimate(
            flops=2 * 1024 * UPPER * chips * count, bytes_accessed=1 << 21, transcendentals=0
        ),
        name="pick_tokens",
    )(ids, table)


def turn_tokens_kernel(place_ref, in_ref, out_ref, square_ref):
    @pl.when(pl.program_id(0) == 0)
    def _():
        square_ref[...] = jnp.zeros_like(square_ref)

    for line in range(2):
        rows = [
            in_ref[t, 0, line, (place_ref[0] + 4 - k) % 4].astype(f32)
            for k in range(4)
            for t in range(4)
        ]
        turned = jnp.concatenate(rows, axis=0).T
        square_ref[...] += turned * turned
        out_ref[:, pl.ds(line * 128, 128)] = turned.astype(bf16)


def turn_tokens(place, stacked):
    count = stacked.shape[-1]
    return pl.pallas_call(
        turn_tokens_kernel,
        grid_spec=pltpu.PrefetchScalarGridSpec(
            num_scalar_prefetch=1,
            grid=(8,),
            in_specs=[pl.BlockSpec((4, 1, 2, 4, 8, count), lambda i, place: (0, i, 0, 0, 0, 0))],
            out_specs=(
                pl.BlockSpec((count, 256), lambda i, place: (0, i)),
                pl.BlockSpec((count, 128), lambda i, place: (0, 0)),
            ),
        ),
        out_shape=(
            jax.ShapeDtypeStruct((count, 2048), bf16),
            jax.ShapeDtypeStruct((count, 128), f32),
        ),
        cost_estimate=pl.CostEstimate(flops=1 << 21, bytes_accessed=1 << 23, transcendentals=0),
        name="turn_tokens",
    )(place, stacked)


def hidden_kernel(group_ref, place_ref, side_ref, square_ref, *refs):
    pieces, (out_ref, rows, sems) = refs[:-3], refs[-3:]
    copies = []
    for piece in pieces:
        for j in range(piece.shape[0]):
            start = pl.multiple_of(place_ref[len(copies)] * 128, 128)
            copies.append(
                pltpu.make_async_copy(piece.at[j], rows.at[pl.ds(start, 128)], sems.at[len(copies)])
            )
            copies[-1].start()
    out_ref[:, WIDTH:] = square_ref[...]
    for copy in copies:
        copy.wait()
    out_ref[:, :WIDTH] = jnp.dot(side_ref[...], rows[...], preferred_element_type=f32)


def partial_hidden(place, group, side, square, pieces):
    total = sum(piece.shape[0] for piece in pieces)
    return pl.pallas_call(
        hidden_kernel,
        grid_spec=pltpu.PrefetchScalarGridSpec(
            num_scalar_prefetch=2,
            grid=(1,),
            in_specs=[
                pl.BlockSpec((TOKENS, 2048), lambda i, group, place: (group[0], 0)),
                pl.BlockSpec((TOKENS, 128), lambda i, group, place: (group[0], 0)),
            ]
            + [pl.BlockSpec(memory_space=pl.ANY)] * len(pieces),
            out_specs=pl.BlockSpec((TOKENS, 1024), lambda i, group, place: (0, 0)),
            scratch_shapes=[VMEM((2048, WIDTH), bf16), pltpu.SemaphoreType.DMA((total,))],
        ),
        out_shape=jax.ShapeDtypeStruct((TOKENS, 1024), f32),
        cost_estimate=pl.CostEstimate(
            flops=2 * TOKENS * 2048 * WIDTH, bytes_accessed=6 << 20, transcendentals=0
        ),
        name="partial_hidden",
    )(group, place, side, square, *pieces)


def label_kernel(own_ref, other_ref, pair_ref, head_ref, out_ref):
    both = own_ref[...] + other_ref[...]
    mean = jnp.sum(both[:, WIDTH:], axis=1, keepdims=True) / 4096.0
    hidden = both[:, :WIDTH] * lax.rsqrt(mean + 1e-05)
    active = hidden / (1.0 + jnp.exp(-hidden))
    pairs = lax.broadcasted_iota(jnp.int32, (PAIRS, TOKENS), 0)
    member = jnp.where(pair_ref[...] == pairs, 1.0, 0.0)
    hot = member.astype(bf16)
    dot = functools.partial(jnp.dot, preferred_element_type=f32)
    first = active.astype(bf16)
    rest = active - first.astype(f32)
    second = rest.astype(bf16)
    third = (rest - second.astype(f32)).astype(bf16)
    totals = dot(hot, first) + (dot(hot, second) + dot(hot, third))
    pooled = (totals / jnp.sum(member, axis=1, keepdims=True)).astype(bf16)
    out_ref[...] = dot(pooled, head_ref[...])


def label_pairs(own, other, pairs, head):
    return pl.pallas_call(
        label_kernel,
        out_shape=jax.ShapeDtypeStruct((PAIRS, 256), f32),
        in_specs=[pl.BlockSpec(memory_space=VMEM)] * 4,
        out_specs=pl.BlockSpec(memory_space=VMEM),
        cost_estimate=pl.CostEstimate(
            flops=2 * 32 * TOKENS * WIDTH, bytes_accessed=3 << 20, transcendentals=TOKENS * WIDTH
        ),
        name="label_pairs",
    )(own, other, pairs, head)


def send_columns(columns):
    got = [columns[0]]
    for hop in range(1, 4):
        got.append(lax.ppermute(columns[hop], "dp", [(i, (i + hop) % 4) for i in range(4)]))
    return jnp.concatenate(got)[None]


def exchange_rows(block):
    count = 8
    up = [(i, i ^ 1) for i in range(count)]
    down = [(i, (i - 1) % count) if i % 2 == 0 else (i, (i + 1) % count) for i in range(count)]
    z, line = lax.axis_index("z"), lax.axis_index("yl")
    sign = 1 - 2 * (z % 2)
    halves = [block, lax.ppermute(block, "yl", [(0, 1), (1, 0)])]
    lines = [line, 1 - line]
    pieces, places = [], []
    last = list(halves)
    for half in range(2):
        pieces.append(halves[half])
        places.append(z * 2 + lines[half])
    for step in range(4):
        for half in range(2):
            got = lax.ppermute(last[half], "z", up if (step + half) % 2 == 0 else down)
            way = sign if half == 0 else -sign
            offsets = ((1,), (-1, -2), (2, 3), (-3, -4))[step]
            pieces.append(got)
            places += [((z + way * k + 16) % count) * 2 + lines[half] for k in offsets]
            last[half] = jnp.concatenate([halves[half], got]) if step == 0 else got
    return pieces, jnp.stack(places).astype(jnp.int32)


def shards(
    master_weight,
    first_moment,
    second_moment,
    teacher_weight,
    grad_parts,
    embed_table,
    token_ids,
    pair_ids,
    class_head,
):
    every_id = lax.all_to_all(
        jnp.broadcast_to(token_ids[None], (32, 1, TOKENS)), ("z", "yl", "c"), 0, 0, tiled=True
    )
    parts = lax.all_to_all(grad_parts.reshape(4, 32, -1), "dp", 0, 0, tiled=True)
    table = turn_table(embed_table)
    picked = pick_tokens(every_id.reshape(16, 1, 2 * TOKENS), table)
    received = lax.all_to_all(
        picked.reshape(64, 8, 2 * TOKENS), ("z", "yl", "dp"), 0, 0, tiled=True
    )
    place = lax.axis_index("dp").astype(jnp.int32).reshape(1)
    master_new, first_new, second_new, teacher_new, columns = optimizer_step(
        place, master_weight, first_moment, second_moment, teacher_weight, parts
    )
    block = send_columns(columns)
    stacked = lax.all_to_all(
        jnp.broadcast_to(received[None], (4, 64, 8, 2 * TOKENS)), "t", 0, 0, tiled=True
    )
    side, square = turn_tokens(place, stacked.reshape(4, 8, 2, 4, 8, 2 * TOKENS))
    pieces, places = exchange_rows(block)
    core = lax.axis_index("c").astype(jnp.int32).reshape(1)
    sent = partial_hidden(places, 1 - core, side, square, pieces)
    other = lax.ppermute(sent, "c", [(0, 1), (1, 0)])
    own = partial_hidden(places, core, side, square, pieces)
    terms = label_pairs(own, other, pair_ids, class_head[0])
    every_term = lax.all_to_all(
        jnp.broadcast_to(terms[None], (16, PAIRS, 256)), ("dp", "t"), 0, 0, tiled=True
    )
    class_logits = jnp.sum(every_term, axis=0, keepdims=True)
    return (master_new, first_new, second_new, teacher_new, class_logits)


def solution(mesh):
    fine = Mesh(mesh.devices.reshape(8, 2, 2, 4, 4), ("z", "yl", "c", "dp", "t"))
    fsdp = ("z", "yl", "c")
    rows = P(fsdp + ("dp",), "t")
    return jax.shard_map(
        shards,
        mesh=fine,
        in_specs=(
            rows,
            rows,
            rows,
            rows,
            P("dp", fsdp, "t"),
            P(fsdp + ("dp", "t"), None),
            P(fsdp, None),
            P(fsdp, None),
            P("t", "dp", None),
        ),
        out_specs=(rows, rows, rows, rows, P(fsdp, None, None)),
        check_vma=False,
    )
```

```python
import functools

import jax
import jax.numpy as jnp
from jax import lax
from jax.experimental import pallas as pl
from jax.experimental.pallas import tpu as pltpu
from jax.sharding import Mesh
from jax.sharding import PartitionSpec as P

PAIRS = 8
TOKENS = 256
WIDTH = 896
UPPER = 512

beta_one = 0.9
beta_two = 0.95
learn_rate = 0.001
decay_rate = 0.1
ema_keep = 0.99

f32 = jnp.float32
bf16 = jnp.bfloat16
VMEM = pltpu.VMEM


def optimizer_kernel(
    master_ref, first_ref, second_ref, teacher_ref, gradient_ref,
    master_out, first_out, second_out, teacher_out, columns_out,
):
    gradient = gradient_ref[...].astype(f32)
    first_full = beta_one * first_ref[...].astype(f32) + (1.0 - beta_one) * gradient
    second_full = (
        beta_two * second_ref[...].astype(f32) + (1.0 - beta_two) * gradient * gradient
    )
    master = master_ref[...]
    master_new = master - learn_rate * (
        first_full / (jnp.sqrt(second_full) + 1e-08) + decay_rate * master
    )
    teacher_new = ema_keep * teacher_ref[...] + (1.0 - ema_keep) * master_new
    master_out[...] = master_new
    first_out[...] = first_full.astype(bf16)
    second_out[...] = second_full.astype(bf16)
    teacher_out[...] = teacher_new
    for line in range(2):
        columns_out[line, 0] = teacher_new.astype(bf16)


def optimizer_step(master_weight, first_moment, second_moment, teacher_weight, gradient):
    block = pl.BlockSpec((32, WIDTH), lambda k: (0, k))
    shape = master_weight.shape
    return pl.pallas_call(
        optimizer_kernel,
        grid=(4,),
        in_specs=[block] * 5,
        out_specs=[block] * 4 + [pl.BlockSpec((2, 1, 32, WIDTH), lambda k: (0, k, 0, 0))],
        out_shape=[
            jax.ShapeDtypeStruct(shape, f32),
            jax.ShapeDtypeStruct(shape, bf16),
            jax.ShapeDtypeStruct(shape, bf16),
            jax.ShapeDtypeStruct(shape, f32),
            jax.ShapeDtypeStruct((2, 4, 32, WIDTH), bf16),
        ],
        cost_estimate=pl.CostEstimate(flops=1 << 21, bytes_accessed=1 << 23, transcendentals=0),
        name="optimizer_step",
    )(master_weight, first_moment, second_moment, teacher_weight, gradient)


def turn_table_kernel(table_ref, out_ref, wide, turned):
    count = table_ref.shape[0]
    wide[pl.ds(0, count)] = table_ref[...].astype(f32)
    wide[pl.ds(count, UPPER - count)] = jnp.zeros((UPPER - count, 8, 128), f32)
    for part in range(UPPER // 128):
        for row in range(8):
            turned[:, row, pl.ds(part * 128, 128)] = wide[pl.ds(part * 128, 128), row, :].T
    out_ref[...] = turned[...].reshape(1024, UPPER).astype(bf16)


def turn_table(table):
    tiles = table.reshape(8, -1, 128).transpose(1, 0, 2)
    return pl.pallas_call(
        turn_table_kernel,
        out_shape=jax.ShapeDtypeStruct((1024, UPPER), bf16),
        in_specs=[pl.BlockSpec(memory_space=VMEM)],
        out_specs=pl.BlockSpec(memory_space=VMEM),
        scratch_shapes=[VMEM((UPPER, 8, 128), f32), VMEM((128, 8, UPPER), f32)],
        cost_estimate=pl.CostEstimate(flops=0, bytes_accessed=1 << 24, transcendentals=0),
        name="turn_table",
    )(tiles)


def pick_kernel(ids_ref, table_ref, out_ref):
    ids = ids_ref[0]
    count = ids.shape[1]
    upper = ids >> 7
    lower = jnp.broadcast_to(ids & 127, (8, count))
    rows = lax.broadcasted_iota(jnp.int32, (UPPER, count), 0)
    hot = jnp.where(rows == upper, 1.0, 0.0).astype(bf16)
    picked = jnp.zeros((8, count), f32)
    for part in range(4):
        lines = jnp.dot(table_ref[pl.ds(part * 256, 256), :], hot, preferred_element_type=f32)
        for k in range(32):
            picked = jnp.where(lower == part * 32 + k, lines[k * 8 : (k + 1) * 8, :], picked)
    for copy in range(out_ref.shape[1]):
        out_ref[0, copy] = picked.astype(bf16)


def pick_tokens(ids, table):
    chips, _, count = ids.shape
    return pl.pallas_call(
        pick_kernel,
        grid=(chips,),
        in_specs=[
            pl.BlockSpec((1, 1, count), lambda i: (i, 0, 0)),
            pl.BlockSpec((1024, UPPER), lambda i: (0, 0)),
        ],
        out_specs=pl.BlockSpec((1, 4, 8, count), lambda i: (i, 0, 0, 0)),
        out_shape=jax.ShapeDtypeStruct((chips, 4, 8, count), bf16),
        cost_estimate=pl.CostEstimate(
            flops=2 * 1024 * UPPER * chips * count, bytes_accessed=1 << 21, transcendentals=0
        ),
        name="pick_tokens",
    )(ids, table)


def turn_tokens_kernel(in_ref, out_ref, square_ref):
    @pl.when(pl.program_id(0) == 0)
    def _():
        square_ref[...] = jnp.zeros_like(square_ref)

    for line in range(2):
        rows = [
            in_ref[t, 0, line, d].astype(f32) for d in range(4) for t in range(4)
        ]
        turned = jnp.concatenate(rows, axis=0).T
        square_ref[...] += turned * turned
        out_ref[:, pl.ds(line * 128, 128)] = turned.astype(bf16)


def turn_tokens(stacked):
    count = stacked.shape[-1]
    return pl.pallas_call(
        turn_tokens_kernel,
        grid=(8,),
        in_specs=[pl.BlockSpec((4, 1, 2, 4, 8, count), lambda i: (0, i, 0, 0, 0, 0))],
        out_specs=(
            pl.BlockSpec((count, 256), lambda i: (0, i)),
            pl.BlockSpec((count, 128), lambda i: (0, 0)),
        ),
        out_shape=(
            jax.ShapeDtypeStruct((count, 2048), bf16),
            jax.ShapeDtypeStruct((count, 128), f32),
        ),
        cost_estimate=pl.CostEstimate(flops=1 << 21, bytes_accessed=1 << 23, transcendentals=0),
        name="turn_tokens",
    )(stacked)


def hidden_kernel(group_ref, side_ref, square_ref, rows_ref, out_ref):
    product = jnp.dot(side_ref[...], rows_ref[...], preferred_element_type=f32)

    @pl.when(pl.program_id(0) == 0)
    def _():
        out_ref[:, :WIDTH] = product
        out_ref[:, WIDTH:] = square_ref[...]

    @pl.when(pl.program_id(0) > 0)
    def _():
        out_ref[:, :WIDTH] += product


def partial_hidden(group, side, square, rows):
    steps = 4
    depth = rows.shape[0] // steps
    return pl.pallas_call(
        hidden_kernel,
        grid_spec=pltpu.PrefetchScalarGridSpec(
            num_scalar_prefetch=1,
            grid=(steps,),
            in_specs=[
                pl.BlockSpec((TOKENS, depth), lambda i, group: (group[0], i)),
                pl.BlockSpec((TOKENS, 128), lambda i, group: (group[0], 0)),
                pl.BlockSpec((depth, WIDTH), lambda i, group: (i, 0)),
            ],
            out_specs=pl.BlockSpec((TOKENS, 1024), lambda i, group: (0, 0)),
        ),
        out_shape=jax.ShapeDtypeStruct((TOKENS, 1024), f32),
        cost_estimate=pl.CostEstimate(
            flops=2 * TOKENS * 2048 * WIDTH, bytes_accessed=6 << 20, transcendentals=0
        ),
        name="partial_hidden",
    )(group, side, square, rows)


def label_kernel(own_ref, other_ref, pair_ref, head_ref, out_ref):
    both = own_ref[...] + other_ref[...]
    mean = jnp.sum(both[:, WIDTH:], axis=1, keepdims=True) / 4096.0
    hidden = both[:, :WIDTH] * lax.rsqrt(mean + 1e-05)
    active = hidden / (1.0 + jnp.exp(-hidden))
    pairs = lax.broadcasted_iota(jnp.int32, (PAIRS, TOKENS), 0)
    member = jnp.where(pair_ref[...] == pairs, 1.0, 0.0)
    hot = member.astype(bf16)
    dot = functools.partial(jnp.dot, preferred_element_type=f32)
    first = active.astype(bf16)
    rest = active - first.astype(f32)
    second = rest.astype(bf16)
    third = (rest - second.astype(f32)).astype(bf16)
    totals = dot(hot, first) + (dot(hot, second) + dot(hot, third))
    pooled = (totals / jnp.sum(member, axis=1, keepdims=True)).astype(bf16)
    out_ref[...] = dot(pooled, head_ref[...])


def label_pairs(own, other, pairs, head):
    return pl.pallas_call(
        label_kernel,
        out_shape=jax.ShapeDtypeStruct((PAIRS, 256), f32),
        in_specs=[pl.BlockSpec(memory_space=VMEM)] * 4,
        out_specs=pl.BlockSpec(memory_space=VMEM),
        cost_estimate=pl.CostEstimate(
            flops=2 * 32 * TOKENS * WIDTH, bytes_accessed=3 << 20, transcendentals=TOKENS * WIDTH
        ),
        name="label_pairs",
    )(own, other, pairs, head)


def shards(
    master_weight,
    first_moment,
    second_moment,
    teacher_weight,
    grad_parts,
    embed_table,
    token_ids,
    pair_ids,
    class_head,
):
    every_id = lax.all_to_all(
        jnp.broadcast_to(token_ids[None], (32, 1, TOKENS)), ("z", "yl", "c"), 0, 0, tiled=True
    )
    gradient = lax.psum_scatter(grad_parts[0], "dp", scatter_dimension=0, tiled=True)
    table = turn_table(embed_table)
    picked = pick_tokens(every_id.reshape(16, 1, 2 * TOKENS), table)
    received = lax.all_to_all(
        picked.reshape(64, 8, 2 * TOKENS), ("z", "yl", "dp"), 0, 0, tiled=True
    )
    master_new, first_new, second_new, teacher_new, columns = optimizer_step(
        master_weight, first_moment, second_moment, teacher_weight, gradient
    )
    block = lax.all_to_all(columns.reshape(8, 32, WIDTH), ("yl", "dp"), 0, 0, tiled=True)
    rows = lax.all_gather(block.reshape(256, WIDTH), "z", axis=0, tiled=True)
    stacked = lax.all_to_all(
        jnp.broadcast_to(received[None], (4, 64, 8, 2 * TOKENS)), "t", 0, 0, tiled=True
    )
    side, square = turn_tokens(stacked.reshape(4, 8, 2, 4, 8, 2 * TOKENS))
    core = lax.axis_index("c").astype(jnp.int32).reshape(1)
    sent = partial_hidden(1 - core, side, square, rows)
    other = lax.ppermute(sent, "c", [(0, 1), (1, 0)])
    own = partial_hidden(core, side, square, rows)
    terms = label_pairs(own, other, pair_ids, class_head[0])
    every_term = lax.all_to_all(
        jnp.broadcast_to(terms[None], (16, PAIRS, 256)), ("dp", "t"), 0, 0, tiled=True
    )
    class_logits = jnp.sum(every_term, axis=0, keepdims=True)
    return (master_new, first_new, second_new, teacher_new, class_logits)


def solution(mesh):
    fine = Mesh(mesh.devices.reshape(8, 2, 2, 4, 4), ("z", "yl", "c", "dp", "t"))
    fsdp = ("z", "yl", "c")
    rows = P(fsdp + ("dp",), "t")
    return jax.shard_map(
        shards,
        mesh=fine,
        in_specs=(
            rows,
            rows,
            rows,
            rows,
            P("dp", fsdp, "t"),
            P(fsdp + ("dp", "t"), None),
            P(fsdp, None),
            P(fsdp, None),
            P("t", "dp", None),
        ),
        out_specs=(rows, rows, rows, rows, P(fsdp, None, None)),
        check_vma=False,
    )
```

```python
import functools

import jax
import jax.numpy as jnp
from jax import lax
from jax.experimental import pallas as pl
from jax.experimental.pallas import tpu as pltpu
from jax.sharding import Mesh
from jax.sharding import PartitionSpec as P

PAIRS = 8
TOKENS = 256
WIDTH = 896
UPPER = 512

beta_one = 0.9
beta_two = 0.95
learn_rate = 0.001
decay_rate = 0.1
ema_keep = 0.99

f32 = jnp.float32
bf16 = jnp.bfloat16
VMEM = pltpu.VMEM


def optimizer_kernel(
    master_ref, first_ref, second_ref, teacher_ref, gradient_ref,
    master_out, first_out, second_out, teacher_out, columns_out,
):
    gradient = gradient_ref[...].astype(f32)
    first_full = beta_one * first_ref[...].astype(f32) + (1.0 - beta_one) * gradient
    second_full = (
        beta_two * second_ref[...].astype(f32) + (1.0 - beta_two) * gradient * gradient
    )
    master = master_ref[...]
    master_new = master - learn_rate * (
        first_full / (jnp.sqrt(second_full) + 1e-08) + decay_rate * master
    )
    teacher_new = ema_keep * teacher_ref[...] + (1.0 - ema_keep) * master_new
    master_out[...] = master_new
    first_out[...] = first_full.astype(bf16)
    second_out[...] = second_full.astype(bf16)
    teacher_out[...] = teacher_new
    for line in range(2):
        columns_out[line, 0] = teacher_new.astype(bf16)


def optimizer_step(master_weight, first_moment, second_moment, teacher_weight, gradient):
    block = pl.BlockSpec((32, WIDTH), lambda k: (0, k))
    shape = master_weight.shape
    return pl.pallas_call(
        optimizer_kernel,
        grid=(4,),
        in_specs=[block] * 5,
        out_specs=[block] * 4 + [pl.BlockSpec((2, 1, 32, WIDTH), lambda k: (0, k, 0, 0))],
        out_shape=[
            jax.ShapeDtypeStruct(shape, f32),
            jax.ShapeDtypeStruct(shape, bf16),
            jax.ShapeDtypeStruct(shape, bf16),
            jax.ShapeDtypeStruct(shape, f32),
            jax.ShapeDtypeStruct((2, 4, 32, WIDTH), bf16),
        ],
        cost_estimate=pl.CostEstimate(flops=1 << 21, bytes_accessed=1 << 23, transcendentals=0),
        name="optimizer_step",
    )(master_weight, first_moment, second_moment, teacher_weight, gradient)


def turn_table_kernel(table_ref, out_ref, wide, turned):
    count = table_ref.shape[0]
    wide[pl.ds(0, count)] = table_ref[...].astype(f32)
    wide[pl.ds(count, UPPER - count)] = jnp.zeros((UPPER - count, 8, 128), f32)
    for part in range(UPPER // 128):
        for row in range(8):
            turned[:, row, pl.ds(part * 128, 128)] = wide[pl.ds(part * 128, 128), row, :].T
    out_ref[...] = turned[...].reshape(1024, UPPER).astype(bf16)


def turn_table(table):
    tiles = table.reshape(8, -1, 128).transpose(1, 0, 2)
    return pl.pallas_call(
        turn_table_kernel,
        out_shape=jax.ShapeDtypeStruct((1024, UPPER), bf16),
        in_specs=[pl.BlockSpec(memory_space=VMEM)],
        out_specs=pl.BlockSpec(memory_space=VMEM),
        scratch_shapes=[VMEM((UPPER, 8, 128), f32), VMEM((128, 8, UPPER), f32)],
        cost_estimate=pl.CostEstimate(flops=0, bytes_accessed=1 << 24, transcendentals=0),
        compiler_params=pltpu.CompilerParams(vmem_limit_bytes=16 << 20),
        name="turn_table",
    )(tiles)


def pick_kernel(ids_ref, table_ref, out_ref):
    ids = ids_ref[0]
    count = ids.shape[1]
    upper = ids >> 7
    lower = jnp.broadcast_to(ids & 127, (8, count))
    rows = lax.broadcasted_iota(jnp.int32, (UPPER, count), 0)
    hot = jnp.where(rows == upper, 1.0, 0.0).astype(bf16)
    picked = jnp.zeros((8, count), f32)
    for part in range(4):
        lines = jnp.dot(table_ref[pl.ds(part * 256, 256), :], hot, preferred_element_type=f32)
        for k in range(32):
            picked = jnp.where(lower == part * 32 + k, lines[k * 8 : (k + 1) * 8, :], picked)
    out_ref[0] = picked.astype(bf16)


def pick_tokens(ids, table):
    chips, _, count = ids.shape
    return pl.pallas_call(
        pick_kernel,
        grid=(chips,),
        in_specs=[
            pl.BlockSpec((1, 1, count), lambda i: (i, 0, 0)),
            pl.BlockSpec((1024, UPPER), lambda i: (0, 0)),
        ],
        out_specs=pl.BlockSpec((1, 8, count), lambda i: (i, 0, 0)),
        out_shape=jax.ShapeDtypeStruct((chips, 8, count), bf16),
        cost_estimate=pl.CostEstimate(
            flops=2 * 1024 * UPPER * chips * count, bytes_accessed=1 << 21, transcendentals=0
        ),
        compiler_params=pltpu.CompilerParams(vmem_limit_bytes=20 << 20),
        name="pick_tokens",
    )(ids, table)


def turn_tokens_kernel(place_ref, in_ref, out_ref, square_ref):
    @pl.when(pl.program_id(0) == 0)
    def _():
        square_ref[...] = jnp.zeros_like(square_ref)

    for line in range(2):
        rows = [
            in_ref[t, place_ref[0] ^ d, 0, line].astype(f32) for d in range(4) for t in range(4)
        ]
        turned = jnp.concatenate(rows, axis=0).T
        square_ref[...] += turned * turned
        out_ref[:, pl.ds(line * 128, 128)] = turned.astype(bf16)


def turn_tokens(place, stacked):
    count = stacked.shape[-1]
    return pl.pallas_call(
        turn_tokens_kernel,
        grid_spec=pltpu.PrefetchScalarGridSpec(
            num_scalar_prefetch=1,
            grid=(8,),
            in_specs=[pl.BlockSpec((4, 4, 1, 2, 8, count), lambda i, place: (0, 0, i, 0, 0, 0))],
            out_specs=(
                pl.BlockSpec((count, 256), lambda i, place: (0, i)),
                pl.BlockSpec((count, 128), lambda i, place: (0, 0)),
            ),
        ),
        out_shape=(
            jax.ShapeDtypeStruct((count, 2048), bf16),
            jax.ShapeDtypeStruct((count, 128), f32),
        ),
        cost_estimate=pl.CostEstimate(flops=1 << 21, bytes_accessed=1 << 23, transcendentals=0),
        name="turn_tokens",
    )(place, stacked)


def hidden_kernel(group_ref, side_ref, square_ref, rows_ref, out_ref):
    product = jnp.dot(side_ref[...], rows_ref[...], preferred_element_type=f32)

    @pl.when(pl.program_id(0) == 0)
    def _():
        out_ref[:, :WIDTH] = product
        out_ref[:, WIDTH:] = square_ref[...]

    @pl.when(pl.program_id(0) > 0)
    def _():
        out_ref[:, :WIDTH] += product


def partial_hidden(group, side, square, rows):
    steps = 4
    depth = rows.shape[0] // steps
    return pl.pallas_call(
        hidden_kernel,
        grid_spec=pltpu.PrefetchScalarGridSpec(
            num_scalar_prefetch=1,
            grid=(steps,),
            in_specs=[
                pl.BlockSpec((TOKENS, depth), lambda i, group: (group[0], i)),
                pl.BlockSpec((TOKENS, 128), lambda i, group: (group[0], 0)),
                pl.BlockSpec((depth, WIDTH), lambda i, group: (i, 0)),
            ],
            out_specs=pl.BlockSpec((TOKENS, 1024), lambda i, group: (0, 0)),
        ),
        out_shape=jax.ShapeDtypeStruct((TOKENS, 1024), f32),
        cost_estimate=pl.CostEstimate(
            flops=2 * TOKENS * 2048 * WIDTH, bytes_accessed=6 << 20, transcendentals=0
        ),
        name="partial_hidden",
    )(group, side, square, rows)


def label_kernel(own_ref, other_ref, pair_ref, head_ref, out_ref):
    both = own_ref[...] + other_ref[...]
    mean = jnp.sum(both[:, WIDTH:], axis=1, keepdims=True) / 4096.0
    hidden = both[:, :WIDTH] * lax.rsqrt(mean + 1e-05)
    active = hidden / (1.0 + jnp.exp(-hidden))
    pairs = lax.broadcasted_iota(jnp.int32, (PAIRS, TOKENS), 0)
    member = jnp.where(pair_ref[...] == pairs, 1.0, 0.0)
    hot = member.astype(bf16)
    dot = functools.partial(jnp.dot, preferred_element_type=f32)
    first = active.astype(bf16)
    rest = active - first.astype(f32)
    second = rest.astype(bf16)
    third = (rest - second.astype(f32)).astype(bf16)
    totals = dot(hot, first) + (dot(hot, second) + dot(hot, third))
    pooled = (totals / jnp.sum(member, axis=1, keepdims=True)).astype(bf16)
    out_ref[...] = dot(pooled, head_ref[...])


def label_pairs(own, other, pairs, head):
    return pl.pallas_call(
        label_kernel,
        out_shape=jax.ShapeDtypeStruct((PAIRS, 256), f32),
        in_specs=[pl.BlockSpec(memory_space=VMEM)] * 4,
        out_specs=pl.BlockSpec(memory_space=VMEM),
        cost_estimate=pl.CostEstimate(
            flops=2 * 32 * TOKENS * WIDTH, bytes_accessed=3 << 20, transcendentals=TOKENS * WIDTH
        ),
        compiler_params=pltpu.CompilerParams(vmem_limit_bytes=16 << 20),
        name="label_pairs",
    )(own, other, pairs, head)


def shards(
    master_weight,
    first_moment,
    second_moment,
    teacher_weight,
    grad_parts,
    embed_table,
    token_ids,
    pair_ids,
    class_head,
):
    every_id = lax.all_to_all(
        jnp.broadcast_to(token_ids[None], (32, 1, TOKENS)), ("z", "yl", "c"), 0, 0, tiled=True
    )
    gradient = lax.psum_scatter(grad_parts[0], "dp", scatter_dimension=0, tiled=True)
    table = turn_table(embed_table)
    picked = pick_tokens(every_id.reshape(16, 1, 2 * TOKENS), table)
    received = lax.all_to_all(
        picked, ("z", "yl"), 0, 0, tiled=True
    )
    master_new, first_new, second_new, teacher_new, columns = optimizer_step(
        master_weight, first_moment, second_moment, teacher_weight, gradient
    )
    block = lax.all_to_all(columns.reshape(8, 32, WIDTH), ("yl", "dp"), 0, 0, tiled=True)
    rows = lax.all_gather(block.reshape(256, WIDTH), "z", axis=0, tiled=True)
    parts = [received]
    for k in (1, 3, 2):
        parts.append(lax.ppermute(received, "dp", [(i, i ^ k) for i in range(4)]))
    near = jnp.stack([parts[0], parts[1], parts[3], parts[2]])
    stacked = lax.all_to_all(
        jnp.broadcast_to(near[None], (4, 4, 16, 8, 2 * TOKENS)), "t", 0, 0, tiled=True
    )
    place = lax.axis_index("dp").astype(jnp.int32).reshape(1)
    side, square = turn_tokens(place, stacked.reshape(4, 4, 8, 2, 8, 2 * TOKENS))
    core = lax.axis_index("c").astype(jnp.int32).reshape(1)
    sent = partial_hidden(1 - core, side, square, rows)
    other = lax.ppermute(sent, "c", [(0, 1), (1, 0)])
    own = partial_hidden(core, side, square, rows)
    terms = label_pairs(own, other, pair_ids, class_head[0])
    every_term = lax.all_to_all(
        jnp.broadcast_to(terms[None], (16, PAIRS, 256)), ("dp", "t"), 0, 0, tiled=True
    )
    class_logits = jnp.sum(every_term, axis=0, keepdims=True)
    return (master_new, first_new, second_new, teacher_new, class_logits)


def solution(mesh):
    fine = Mesh(mesh.devices.reshape(8, 2, 2, 4, 4), ("z", "yl", "c", "dp", "t"))
    fsdp = ("z", "yl", "c")
    rows = P(fsdp + ("dp",), "t")
    return jax.shard_map(
        shards,
        mesh=fine,
        in_specs=(
            rows,
            rows,
            rows,
            rows,
            P("dp", fsdp, "t"),
            P(fsdp + ("dp", "t"), None),
            P(fsdp, None),
            P(fsdp, None),
            P("t", "dp", None),
        ),
        out_specs=(rows, rows, rows, rows, P(fsdp, None, None)),
        check_vma=False,
    )
```

```python
import functools

import jax
import jax.numpy as jnp
from jax import lax
from jax.experimental import pallas as pl
from jax.experimental.pallas import tpu as pltpu
from jax.sharding import Mesh
from jax.sharding import PartitionSpec as P

PAIRS = 8
TOKENS = 256
WIDTH = 896
UPPER = 512

beta_one = 0.9
beta_two = 0.95
learn_rate = 0.001
decay_rate = 0.1
ema_keep = 0.99

f32 = jnp.float32
bf16 = jnp.bfloat16
VMEM = pltpu.VMEM


def optimizer_kernel(
    master_ref, first_ref, second_ref, teacher_ref, gradient_ref,
    master_out, first_out, second_out, teacher_out, columns_out,
):
    gradient = gradient_ref[...].astype(f32)
    first_full = beta_one * first_ref[...].astype(f32) + (1.0 - beta_one) * gradient
    second_full = (
        beta_two * second_ref[...].astype(f32) + (1.0 - beta_two) * gradient * gradient
    )
    master = master_ref[...]
    master_new = master - learn_rate * (
        first_full / (jnp.sqrt(second_full) + 1e-08) + decay_rate * master
    )
    teacher_new = ema_keep * teacher_ref[...] + (1.0 - ema_keep) * master_new
    master_out[...] = master_new
    first_out[...] = first_full.astype(bf16)
    second_out[...] = second_full.astype(bf16)
    teacher_out[...] = teacher_new
    for line in range(2):
        columns_out[line, 0] = teacher_new.astype(bf16)


def optimizer_step(master_weight, first_moment, second_moment, teacher_weight, gradient):
    block = pl.BlockSpec((32, WIDTH), lambda k: (0, k))
    shape = master_weight.shape
    return pl.pallas_call(
        optimizer_kernel,
        grid=(4,),
        in_specs=[block] * 5,
        out_specs=[block] * 4 + [pl.BlockSpec((2, 1, 32, WIDTH), lambda k: (0, k, 0, 0))],
        out_shape=[
            jax.ShapeDtypeStruct(shape, f32),
            jax.ShapeDtypeStruct(shape, bf16),
            jax.ShapeDtypeStruct(shape, bf16),
            jax.ShapeDtypeStruct(shape, f32),
            jax.ShapeDtypeStruct((2, 4, 32, WIDTH), bf16),
        ],
        cost_estimate=pl.CostEstimate(flops=1 << 21, bytes_accessed=1 << 23, transcendentals=0),
        compiler_params=pltpu.CompilerParams(vmem_limit_bytes=16 << 20),
        name="optimizer_step",
    )(
        master_weight, first_moment, second_moment, teacher_weight,
        pltpu.with_memory_space_constraint(gradient, pltpu.HBM),
    )


def turn_table_kernel(table_ref, out_ref, wide, turned):
    count = table_ref.shape[0]
    wide[pl.ds(0, count)] = table_ref[...].astype(f32)
    wide[pl.ds(count, UPPER - count)] = jnp.zeros((UPPER - count, 8, 128), f32)
    for part in range(UPPER // 128):
        for row in range(8):
            turned[:, row, pl.ds(part * 128, 128)] = wide[pl.ds(part * 128, 128), row, :].T
    out_ref[...] = turned[...].reshape(1024, UPPER).astype(bf16)


def turn_table(table):
    tiles = table.reshape(8, -1, 128).transpose(1, 0, 2)
    return pl.pallas_call(
        turn_table_kernel,
        out_shape=jax.ShapeDtypeStruct((1024, UPPER), bf16),
        in_specs=[pl.BlockSpec(memory_space=VMEM)],
        out_specs=pl.BlockSpec(memory_space=VMEM),
        scratch_shapes=[VMEM((UPPER, 8, 128), f32), VMEM((128, 8, UPPER), f32)],
        cost_estimate=pl.CostEstimate(flops=0, bytes_accessed=1 << 24, transcendentals=0),
        compiler_params=pltpu.CompilerParams(vmem_limit_bytes=16 << 20),
        name="turn_table",
    )(tiles)


def pick_kernel(ids_ref, table_ref, out_ref):
    ids = ids_ref[0]
    count = ids.shape[1]
    upper = ids >> 7
    lower = jnp.broadcast_to(ids & 127, (8, count))
    rows = lax.broadcasted_iota(jnp.int32, (UPPER, count), 0)
    hot = jnp.where(rows == upper, 1.0, 0.0).astype(bf16)
    picked = jnp.zeros((8, count), f32)
    for part in range(4):
        lines = jnp.dot(table_ref[pl.ds(part * 256, 256), :], hot, preferred_element_type=f32)
        for k in range(32):
            picked = jnp.where(lower == part * 32 + k, lines[k * 8 : (k + 1) * 8, :], picked)
    out_ref[0] = picked.astype(bf16)


def pick_tokens(ids, table):
    chips, _, count = ids.shape
    return pl.pallas_call(
        pick_kernel,
        grid=(chips,),
        in_specs=[
            pl.BlockSpec((1, 1, count), lambda i: (i, 0, 0)),
            pl.BlockSpec((1024, UPPER), lambda i: (0, 0)),
        ],
        out_specs=pl.BlockSpec((1, 8, count), lambda i: (i, 0, 0)),
        out_shape=jax.ShapeDtypeStruct((chips, 8, count), bf16),
        cost_estimate=pl.CostEstimate(
            flops=2 * 1024 * UPPER * chips * count, bytes_accessed=1 << 21, transcendentals=0
        ),
        compiler_params=pltpu.CompilerParams(vmem_limit_bytes=20 << 20),
        name="pick_tokens",
    )(ids, table)


def turn_tokens_kernel(place_ref, in_ref, out_ref):
    for pair in range(4):
        rows = [
            in_ref[place_ref[0] ^ d, pair * 4 + line].astype(f32)
            for line in range(4)
            for d in range(4)
        ]
        turned = jnp.concatenate(rows, axis=0).T.astype(bf16)
        for copy in range(4):
            out_ref[copy, :, pair * 128 : (pair + 1) * 128] = turned


def turn_tokens(place, near):
    count = near.shape[-1]
    return pl.pallas_call(
        turn_tokens_kernel,
        grid_spec=pltpu.PrefetchScalarGridSpec(
            num_scalar_prefetch=1,
            grid=(1,),
            in_specs=[pl.BlockSpec((4, 16, 8, count), lambda i, place: (0, 0, 0, 0))],
            out_specs=pl.BlockSpec((4, count, 512), lambda i, place: (0, 0, 0)),
        ),
        out_shape=jax.ShapeDtypeStruct((4, count, 512), bf16),
        cost_estimate=pl.CostEstimate(flops=1 << 21, bytes_accessed=1 << 22, transcendentals=0),
        name="turn_tokens",
    )(place, near)


def hidden_kernel(group_ref, side_ref, rows_ref, out_ref):
    side = side_ref[0]
    product = jnp.dot(side, rows_ref[...].reshape(512, WIDTH), preferred_element_type=f32)
    wide = side.astype(f32)
    square = wide * wide
    square = (square[:, :128] + square[:, 128:256]) + (square[:, 256:384] + square[:, 384:])

    @pl.when(pl.program_id(0) == 0)
    def _():
        out_ref[:, :WIDTH] = product
        out_ref[:, WIDTH:] = square

    @pl.when(pl.program_id(0) > 0)
    def _():
        out_ref[:, :WIDTH] += product
        out_ref[:, WIDTH:] += square


def partial_hidden(group, side, rows):
    return pl.pallas_call(
        hidden_kernel,
        grid_spec=pltpu.PrefetchScalarGridSpec(
            num_scalar_prefetch=1,
            grid=(4,),
            in_specs=[
                pl.BlockSpec((1, TOKENS, 512), lambda t, group: (t, group[0], 0)),
                pl.BlockSpec((8, 1, 64, WIDTH), lambda t, group: (0, t, 0, 0)),
            ],
            out_specs=pl.BlockSpec((TOKENS, 1024), lambda t, group: (0, 0)),
        ),
        out_shape=jax.ShapeDtypeStruct((TOKENS, 1024), f32),
        cost_estimate=pl.CostEstimate(
            flops=2 * TOKENS * 2048 * WIDTH, bytes_accessed=6 << 20, transcendentals=0
        ),
        compiler_params=pltpu.CompilerParams(vmem_limit_bytes=24 << 20),
        name="partial_hidden",
    )(group, side, pltpu.with_memory_space_constraint(rows, pltpu.HBM))


def label_kernel(own_ref, other_ref, pair_ref, head_ref, out_ref):
    both = own_ref[...] + other_ref[...]
    mean = jnp.sum(both[:, WIDTH:], axis=1, keepdims=True) / 4096.0
    hidden = both[:, :WIDTH] * lax.rsqrt(mean + 1e-05)
    active = hidden / (1.0 + jnp.exp(-hidden))
    pairs = lax.broadcasted_iota(jnp.int32, (PAIRS, TOKENS), 0)
    member = jnp.where(pair_ref[...] == pairs, 1.0, 0.0)
    hot = member.astype(bf16)
    dot = functools.partial(jnp.dot, preferred_element_type=f32)
    first = active.astype(bf16)
    rest = active - first.astype(f32)
    second = rest.astype(bf16)
    third = (rest - second.astype(f32)).astype(bf16)
    totals = dot(hot, first) + (dot(hot, second) + dot(hot, third))
    pooled = (totals / jnp.sum(member, axis=1, keepdims=True)).astype(bf16)
    out_ref[...] = dot(pooled, head_ref[...])


def label_pairs(own, other, pairs, head):
    return pl.pallas_call(
        label_kernel,
        out_shape=jax.ShapeDtypeStruct((PAIRS, 256), f32),
        in_specs=[pl.BlockSpec(memory_space=VMEM)] * 4,
        out_specs=pl.BlockSpec(memory_space=VMEM),
        cost_estimate=pl.CostEstimate(
            flops=2 * 32 * TOKENS * WIDTH, bytes_accessed=3 << 20, transcendentals=TOKENS * WIDTH
        ),
        compiler_params=pltpu.CompilerParams(vmem_limit_bytes=16 << 20),
        name="label_pairs",
    )(own, other, pairs, head)


def shards(
    master_weight,
    first_moment,
    second_moment,
    teacher_weight,
    grad_parts,
    embed_table,
    token_ids,
    pair_ids,
    class_head,
):
    every_id = lax.all_to_all(
        jnp.broadcast_to(token_ids[None], (32, 1, TOKENS)), ("z", "yl", "c"), 0, 0, tiled=True
    )
    gradient = lax.psum_scatter(grad_parts[0], "dp", scatter_dimension=0, tiled=True)
    table = turn_table(embed_table)
    picked = pick_tokens(every_id.reshape(16, 1, 2 * TOKENS), table)
    received = lax.all_to_all(
        picked, ("z", "yl"), 0, 0, tiled=True
    )
    master_new, first_new, second_new, teacher_new, columns = optimizer_step(
        master_weight, first_moment, second_moment, teacher_weight, gradient
    )
    block = lax.all_to_all(columns.reshape(8, 32, WIDTH), ("yl", "dp"), 0, 0, tiled=True)
    sorted_block = block.reshape(8, 4, 8, WIDTH).transpose(1, 0, 2, 3).reshape(256, WIDTH)
    rows = lax.all_gather(sorted_block, "z", axis=0, tiled=True)
    parts = [received]
    for k in (1, 3, 2):
        parts.append(lax.ppermute(received, "dp", [(i, i ^ k) for i in range(4)]))
    near = jnp.stack([parts[0], parts[1], parts[3], parts[2]])
    place = lax.axis_index("dp").astype(jnp.int32).reshape(1)
    turned = turn_tokens(place, near)
    side = lax.all_to_all(turned, "t", 0, 0, tiled=True)
    rows = rows.reshape(8, 4, 64, WIDTH)
    core = lax.axis_index("c").astype(jnp.int32).reshape(1)
    sent = partial_hidden(1 - core, side, rows)
    other = lax.ppermute(sent, "c", [(0, 1), (1, 0)])
    own = partial_hidden(core, side, rows)
    terms = label_pairs(own, other, pair_ids, class_head[0])
    every_term = lax.all_to_all(
        jnp.broadcast_to(terms[None], (16, PAIRS, 256)), ("dp", "t"), 0, 0, tiled=True
    )
    class_logits = jnp.sum(every_term, axis=0, keepdims=True)
    return (master_new, first_new, second_new, teacher_new, class_logits)


def solution(mesh):
    fine = Mesh(mesh.devices.reshape(8, 2, 2, 4, 4), ("z", "yl", "c", "dp", "t"))
    fsdp = ("z", "yl", "c")
    rows = P(fsdp + ("dp",), "t")
    return jax.shard_map(
        shards,
        mesh=fine,
        in_specs=(
            rows,
            rows,
            rows,
            rows,
            P("dp", fsdp, "t"),
            P(fsdp + ("dp", "t"), None),
            P(fsdp, None),
            P(fsdp, None),
            P("t", "dp", None),
        ),
        out_specs=(rows, rows, rows, rows, P(fsdp, None, None)),
        check_vma=False,
    )
```

```python
import functools

import jax
import jax.numpy as jnp
from jax import lax
from jax.experimental import pallas as pl
from jax.experimental.pallas import tpu as pltpu
from jax.sharding import Mesh
from jax.sharding import PartitionSpec as P

PAIRS = 8
TOKENS = 256
WIDTH = 896
UPPER = 512

beta_one = 0.9
beta_two = 0.95
learn_rate = 0.001
decay_rate = 0.1
ema_keep = 0.99

f32 = jnp.float32
bf16 = jnp.bfloat16
VMEM = pltpu.VMEM


def updated(master_ref, first_ref, second_ref, teacher_ref, gradient_ref):
    gradient = gradient_ref[...].astype(f32)
    first_full = beta_one * first_ref[...].astype(f32) + (1.0 - beta_one) * gradient
    second_full = (
        beta_two * second_ref[...].astype(f32) + (1.0 - beta_two) * gradient * gradient
    )
    master = master_ref[...]
    master_new = master - learn_rate * (
        first_full / (jnp.sqrt(second_full) + 1e-08) + decay_rate * master
    )
    teacher_new = ema_keep * teacher_ref[...] + (1.0 - ema_keep) * master_new
    return master_new, first_full, second_full, teacher_new


def columns_kernel(master_ref, first_ref, second_ref, teacher_ref, gradient_ref, columns_out):
    teacher = updated(master_ref, first_ref, second_ref, teacher_ref, gradient_ref)[3]
    for line in range(2):
        columns_out[line, 0] = teacher.astype(bf16)


def optimizer_kernel(
    master_ref, first_ref, second_ref, teacher_ref, gradient_ref,
    master_out, first_out, second_out, teacher_out,
):
    master, first, second, teacher = updated(
        master_ref, first_ref, second_ref, teacher_ref, gradient_ref
    )
    master_out[...] = master
    first_out[...] = first.astype(bf16)
    second_out[...] = second.astype(bf16)
    teacher_out[...] = teacher


BLOCK = pl.BlockSpec((32, WIDTH), lambda k: (0, k))
UPDATE = dict(
    grid=(4,),
    in_specs=[BLOCK] * 5,
    cost_estimate=pl.CostEstimate(flops=1 << 21, bytes_accessed=1 << 22, transcendentals=0),
    compiler_params=pltpu.CompilerParams(vmem_limit_bytes=16 << 20),
)


def teacher_columns(*state):
    return pl.pallas_call(
        columns_kernel,
        out_specs=pl.BlockSpec((2, 1, 32, WIDTH), lambda k: (0, k, 0, 0)),
        out_shape=jax.ShapeDtypeStruct((2, 4, 32, WIDTH), bf16),
        name="teacher_columns",
        **UPDATE,
    )(*state)


def optimizer_step(*state):
    shape = state[0].shape
    return pl.pallas_call(
        optimizer_kernel,
        out_specs=[BLOCK] * 4,
        out_shape=[jax.ShapeDtypeStruct(shape, kind) for kind in (f32, bf16, bf16, f32)],
        name="optimizer_step",
        **UPDATE,
    )(*state)


def turn_table_kernel(table_ref, out_ref, wide, turned):
    count = table_ref.shape[0]
    wide[pl.ds(0, count)] = table_ref[...].astype(f32)
    wide[pl.ds(count, UPPER - count)] = jnp.zeros((UPPER - count, 8, 128), f32)
    for part in range(UPPER // 128):
        for row in range(8):
            turned[:, row, pl.ds(part * 128, 128)] = wide[pl.ds(part * 128, 128), row, :].T
    out_ref[...] = turned[...].reshape(1024, UPPER).astype(bf16)


def turn_table(table):
    tiles = table.reshape(8, -1, 128).transpose(1, 0, 2)
    return pl.pallas_call(
        turn_table_kernel,
        out_shape=jax.ShapeDtypeStruct((1024, UPPER), bf16),
        in_specs=[pl.BlockSpec(memory_space=VMEM)],
        out_specs=pl.BlockSpec(memory_space=VMEM),
        scratch_shapes=[VMEM((UPPER, 8, 128), f32), VMEM((128, 8, UPPER), f32)],
        cost_estimate=pl.CostEstimate(flops=0, bytes_accessed=1 << 24, transcendentals=0),
        compiler_params=pltpu.CompilerParams(vmem_limit_bytes=16 << 20),
        name="turn_table",
    )(tiles)


def pick_kernel(ids_ref, table_ref, out_ref):
    ids = jnp.concatenate([ids_ref[0], ids_ref[1]], axis=1)
    count = ids.shape[1]
    upper = ids >> 7
    lower = jnp.broadcast_to(ids & 127, (8, count))
    rows = lax.broadcasted_iota(jnp.int32, (UPPER, count), 0)
    hot = jnp.where(rows == upper, 1.0, 0.0).astype(bf16)
    picked = jnp.zeros((8, count), f32)
    for part in range(4):
        lines = jnp.dot(table_ref[pl.ds(part * 256, 256), :], hot, preferred_element_type=f32)
        for k in range(32):
            picked = jnp.where(lower == part * 32 + k, lines[k * 8 : (k + 1) * 8, :], picked)
    out_ref[0] = picked.astype(bf16)


def pick_tokens(ids, table):
    chips, count = ids.shape[0] // 2, 2 * ids.shape[2]
    return pl.pallas_call(
        pick_kernel,
        grid=(chips,),
        in_specs=[
            pl.BlockSpec((2, 1, TOKENS), lambda i: (i, 0, 0)),
            pl.BlockSpec((1024, UPPER), lambda i: (0, 0)),
        ],
        out_specs=pl.BlockSpec((1, 8, count), lambda i: (i, 0, 0)),
        out_shape=jax.ShapeDtypeStruct((chips, 8, count), bf16),
        cost_estimate=pl.CostEstimate(
            flops=2 * 1024 * UPPER * chips * count, bytes_accessed=1 << 21, transcendentals=0
        ),
        compiler_params=pltpu.CompilerParams(vmem_limit_bytes=20 << 20),
        name="pick_tokens",
    )(ids, table)


def turn_tokens_kernel(place_ref, in_ref, out_ref):
    for pair in range(4):
        rows = [
            in_ref[place_ref[0] ^ d, pair * 4 + line].astype(f32)
            for line in range(4)
            for d in range(4)
        ]
        turned = jnp.concatenate(rows, axis=0).T.astype(bf16)
        for copy in range(4):
            out_ref[copy, :, pair * 128 : (pair + 1) * 128] = turned


def turn_tokens(place, near):
    count = near.shape[-1]
    return pl.pallas_call(
        turn_tokens_kernel,
        grid_spec=pltpu.PrefetchScalarGridSpec(
            num_scalar_prefetch=1,
            grid=(1,),
            in_specs=[pl.BlockSpec((4, 16, 8, count), lambda i, place: (0, 0, 0, 0))],
            out_specs=pl.BlockSpec((4, count, 512), lambda i, place: (0, 0, 0)),
        ),
        out_shape=jax.ShapeDtypeStruct((4, count, 512), bf16),
        cost_estimate=pl.CostEstimate(flops=1 << 21, bytes_accessed=1 << 22, transcendentals=0),
        name="turn_tokens",
    )(place, near)


def hidden_kernel(group_ref, side_ref, rows_ref, out_ref):
    side = side_ref[0]
    product = jnp.dot(side, rows_ref[...].reshape(512, WIDTH), preferred_element_type=f32)
    wide = side.astype(f32)
    square = wide * wide
    square = (square[:, :128] + square[:, 128:256]) + (square[:, 256:384] + square[:, 384:])

    @pl.when(pl.program_id(0) == 0)
    def _():
        out_ref[:, :WIDTH] = product
        out_ref[:, WIDTH:] = square

    @pl.when(pl.program_id(0) > 0)
    def _():
        out_ref[:, :WIDTH] += product
        out_ref[:, WIDTH:] += square


def partial_hidden(group, side, rows):
    return pl.pallas_call(
        hidden_kernel,
        grid_spec=pltpu.PrefetchScalarGridSpec(
            num_scalar_prefetch=1,
            grid=(4,),
            in_specs=[
                pl.BlockSpec((1, TOKENS, 512), lambda t, group: (t, group[0], 0)),
                pl.BlockSpec((8, 1, 64, WIDTH), lambda t, group: (0, t, 0, 0)),
            ],
            out_specs=pl.BlockSpec((TOKENS, 1024), lambda t, group: (0, 0)),
        ),
        out_shape=jax.ShapeDtypeStruct((TOKENS, 1024), f32),
        cost_estimate=pl.CostEstimate(
            flops=2 * TOKENS * 2048 * WIDTH, bytes_accessed=6 << 20, transcendentals=0
        ),
        compiler_params=pltpu.CompilerParams(vmem_limit_bytes=24 << 20),
        name="partial_hidden",
    )(group, side, pltpu.with_memory_space_constraint(rows, pltpu.HBM))


def label_kernel(own_ref, other_ref, pair_ref, head_ref, out_ref):
    both = own_ref[...] + other_ref[...]
    mean = jnp.sum(both[:, WIDTH:], axis=1, keepdims=True) / 4096.0
    hidden = both[:, :WIDTH] * lax.rsqrt(mean + 1e-05)
    active = hidden / (1.0 + jnp.exp(-hidden))
    pairs = lax.broadcasted_iota(jnp.int32, (PAIRS, TOKENS), 0)
    member = jnp.where(pair_ref[...] == pairs, 1.0, 0.0)
    hot = member.astype(bf16)
    dot = functools.partial(jnp.dot, preferred_element_type=f32)
    first = active.astype(bf16)
    rest = active - first.astype(f32)
    second = rest.astype(bf16)
    third = (rest - second.astype(f32)).astype(bf16)
    totals = dot(hot, first) + (dot(hot, second) + dot(hot, third))
    pooled = (totals / jnp.sum(member, axis=1, keepdims=True)).astype(bf16)
    out_ref[...] = dot(pooled, head_ref[...])


def label_pairs(own, other, pairs, head):
    return pl.pallas_call(
        label_kernel,
        out_shape=jax.ShapeDtypeStruct((PAIRS, 256), f32),
        in_specs=[pl.BlockSpec(memory_space=VMEM)] * 4,
        out_specs=pl.BlockSpec(memory_space=VMEM),
        cost_estimate=pl.CostEstimate(
            flops=2 * 32 * TOKENS * WIDTH, bytes_accessed=3 << 20, transcendentals=TOKENS * WIDTH
        ),
        compiler_params=pltpu.CompilerParams(vmem_limit_bytes=16 << 20),
        name="label_pairs",
    )(own, other, pairs, head)


def shards(
    master_weight,
    first_moment,
    second_moment,
    teacher_weight,
    grad_parts,
    embed_table,
    token_ids,
    pair_ids,
    class_head,
):
    every_id = lax.all_to_all(
        jnp.broadcast_to(token_ids[None], (32, 1, TOKENS)), ("z", "yl", "c"), 0, 0, tiled=True
    )
    gradient = lax.psum_scatter(grad_parts[0], "dp", scatter_dimension=0, tiled=True)
    table = turn_table(embed_table)
    picked = pick_tokens(every_id, table)
    received = lax.all_to_all(
        picked, ("z", "yl"), 0, 0, tiled=True
    )
    state = (
        master_weight, first_moment, second_moment, teacher_weight,
        pltpu.with_memory_space_constraint(gradient, pltpu.HBM),
    )
    columns = teacher_columns(*state)
    master_new, first_new, second_new, teacher_new = optimizer_step(*state)
    block = lax.all_to_all(columns.reshape(8, 32, WIDTH), ("yl", "dp"), 0, 0, tiled=True)
    sorted_block = block.reshape(8, 4, 8, WIDTH).transpose(1, 0, 2, 3).reshape(256, WIDTH)
    rows = lax.all_gather(sorted_block, "z", axis=0, tiled=True)
    parts = [received]
    for k in (1, 3, 2):
        parts.append(lax.ppermute(received, "dp", [(i, i ^ k) for i in range(4)]))
    near = jnp.stack([parts[0], parts[1], parts[3], parts[2]])
    place = lax.axis_index("dp").astype(jnp.int32).reshape(1)
    turned = turn_tokens(place, near)
    side = lax.all_to_all(turned, "t", 0, 0, tiled=True)
    rows = rows.reshape(8, 4, 64, WIDTH)
    core = lax.axis_index("c").astype(jnp.int32).reshape(1)
    sent = partial_hidden(1 - core, side, rows)
    other = lax.ppermute(sent, "c", [(0, 1), (1, 0)])
    own = partial_hidden(core, side, rows)
    terms = label_pairs(own, other, pair_ids, class_head[0])
    every_term = lax.all_to_all(
        jnp.broadcast_to(terms[None], (16, PAIRS, 256)), ("dp", "t"), 0, 0, tiled=True
    )
    class_logits = jnp.sum(every_term, axis=0, keepdims=True)
    return (master_new, first_new, second_new, teacher_new, class_logits)


def solution(mesh):
    fine = Mesh(mesh.devices.reshape(8, 2, 2, 4, 4), ("z", "yl", "c", "dp", "t"))
    fsdp = ("z", "yl", "c")
    rows = P(fsdp + ("dp",), "t")
    return jax.shard_map(
        shards,
        mesh=fine,
        in_specs=(
            rows,
            rows,
            rows,
            rows,
            P("dp", fsdp, "t"),
            P(fsdp + ("dp", "t"), None),
            P(fsdp, None),
            P(fsdp, None),
            P("t", "dp", None),
        ),
        out_specs=(rows, rows, rows, rows, P(fsdp, None, None)),
        check_vma=False,
    )
```

```python
import functools

import jax
import jax.numpy as jnp
from jax import lax
from jax.experimental import pallas as pl
from jax.experimental.pallas import tpu as pltpu
from jax.sharding import Mesh
from jax.sharding import PartitionSpec as P

PAIRS = 8
TOKENS = 256
WIDTH = 896
UPPER = 512

beta_one = 0.9
beta_two = 0.95
learn_rate = 0.001
decay_rate = 0.1
ema_keep = 0.99

f32 = jnp.float32
bf16 = jnp.bfloat16
VMEM = pltpu.VMEM


def updated(master_ref, first_ref, second_ref, teacher_ref, gradient_ref):
    gradient = gradient_ref[...].astype(f32)
    first_full = beta_one * first_ref[...].astype(f32) + (1.0 - beta_one) * gradient
    second_full = (
        beta_two * second_ref[...].astype(f32) + (1.0 - beta_two) * gradient * gradient
    )
    master = master_ref[...]
    master_new = master - learn_rate * (
        first_full / (jnp.sqrt(second_full) + 1e-08) + decay_rate * master
    )
    teacher_new = ema_keep * teacher_ref[...] + (1.0 - ema_keep) * master_new
    return master_new, first_full, second_full, teacher_new


def columns_kernel(master_ref, first_ref, second_ref, teacher_ref, gradient_ref, columns_out):
    teacher = updated(master_ref, first_ref, second_ref, teacher_ref, gradient_ref)[3]
    for line in range(2):
        columns_out[line, 0] = teacher.astype(bf16)


def optimizer_kernel(
    master_ref, first_ref, second_ref, teacher_ref, gradient_ref,
    master_out, first_out, second_out, teacher_out,
):
    master, first, second, teacher = updated(
        master_ref, first_ref, second_ref, teacher_ref, gradient_ref
    )
    master_out[...] = master
    first_out[...] = first.astype(bf16)
    second_out[...] = second.astype(bf16)
    teacher_out[...] = teacher


BLOCK = pl.BlockSpec((32, WIDTH), lambda k: (0, k))
UPDATE = dict(
    grid=(4,),
    in_specs=[BLOCK] * 5,
    cost_estimate=pl.CostEstimate(flops=1 << 21, bytes_accessed=1 << 22, transcendentals=0),
    compiler_params=pltpu.CompilerParams(vmem_limit_bytes=16 << 20),
)


def teacher_columns(*state):
    return pl.pallas_call(
        columns_kernel,
        out_specs=pl.BlockSpec((2, 1, 32, WIDTH), lambda k: (0, k, 0, 0)),
        out_shape=jax.ShapeDtypeStruct((2, 4, 32, WIDTH), bf16),
        name="teacher_columns",
        **UPDATE,
    )(*state)


def optimizer_step(*state):
    shape = state[0].shape
    return pl.pallas_call(
        optimizer_kernel,
        out_specs=[BLOCK] * 4,
        out_shape=[jax.ShapeDtypeStruct(shape, kind) for kind in (f32, bf16, bf16, f32)],
        name="optimizer_step",
        **UPDATE,
    )(*state)


def turn_table_kernel(table_ref, out_ref, wide, turned):
    count = table_ref.shape[0]
    wide[pl.ds(0, count)] = table_ref[...].astype(f32)
    wide[pl.ds(count, UPPER - count)] = jnp.zeros((UPPER - count, 8, 128), f32)
    for part in range(UPPER // 128):
        for row in range(8):
            turned[:, row, pl.ds(part * 128, 128)] = wide[pl.ds(part * 128, 128), row, :].T
    out_ref[...] = turned[...].reshape(1024, UPPER).astype(bf16)


def turn_table(table):
    tiles = table.reshape(8, -1, 128).transpose(1, 0, 2)
    return pl.pallas_call(
        turn_table_kernel,
        out_shape=jax.ShapeDtypeStruct((1024, UPPER), bf16),
        in_specs=[pl.BlockSpec(memory_space=VMEM)],
        out_specs=pl.BlockSpec(memory_space=VMEM),
        scratch_shapes=[VMEM((UPPER, 8, 128), f32), VMEM((128, 8, UPPER), f32)],
        cost_estimate=pl.CostEstimate(flops=0, bytes_accessed=1 << 24, transcendentals=0),
        compiler_params=pltpu.CompilerParams(vmem_limit_bytes=16 << 20),
        name="turn_table",
    )(tiles)


def pick_kernel(ids_ref, table_ref, out_ref):
    groups = ids_ref.shape[0]
    ids = jnp.concatenate([ids_ref[group] for group in range(groups)], axis=1)
    count = ids.shape[1]
    upper = ids >> 7
    lower = jnp.broadcast_to(ids & 127, (8, count))
    rows = lax.broadcasted_iota(jnp.int32, (UPPER, count), 0)
    hot = jnp.where(rows == upper, 1.0, 0.0).astype(bf16)
    lines = jnp.dot(table_ref[...], hot, preferred_element_type=f32)
    picked = jnp.zeros((8, count), f32)
    for k in range(128):
        picked = jnp.where(lower == k, lines[k * 8 : (k + 1) * 8, :], picked)
    width = out_ref.shape[2]
    for chip in range(out_ref.shape[0]):
        out_ref[chip] = picked[:, chip * width : (chip + 1) * width].astype(bf16)


def pick_tokens(ids, table):
    groups, width = 16, 2 * TOKENS
    chips, steps = ids.shape[0] // 2, ids.shape[0] // groups
    return pl.pallas_call(
        pick_kernel,
        grid=(steps,),
        in_specs=[
            pl.BlockSpec((groups, 1, TOKENS), lambda i: (i, 0, 0)),
            pl.BlockSpec((1024, UPPER), lambda i: (0, 0)),
        ],
        out_specs=pl.BlockSpec((groups // 2, 8, width), lambda i: (i, 0, 0)),
        out_shape=jax.ShapeDtypeStruct((chips, 8, width), bf16),
        cost_estimate=pl.CostEstimate(
            flops=2 * 1024 * UPPER * chips * width, bytes_accessed=1 << 21, transcendentals=0
        ),
        compiler_params=pltpu.CompilerParams(vmem_limit_bytes=40 << 20),
        name="pick_tokens",
    )(ids, table)


def turn_tokens_kernel(place_ref, in_ref, out_ref):
    for pair in range(4):
        rows = [
            in_ref[place_ref[0] ^ d, pair * 4 + line].astype(f32)
            for line in range(4)
            for d in range(4)
        ]
        turned = jnp.concatenate(rows, axis=0).T.astype(bf16)
        for copy in range(4):
            out_ref[copy, :, pair * 128 : (pair + 1) * 128] = turned


def turn_tokens(place, near):
    count = near.shape[-1]
    return pl.pallas_call(
        turn_tokens_kernel,
        grid_spec=pltpu.PrefetchScalarGridSpec(
            num_scalar_prefetch=1,
            grid=(1,),
            in_specs=[pl.BlockSpec((4, 16, 8, count), lambda i, place: (0, 0, 0, 0))],
            out_specs=pl.BlockSpec((4, count, 512), lambda i, place: (0, 0, 0)),
        ),
        out_shape=jax.ShapeDtypeStruct((4, count, 512), bf16),
        cost_estimate=pl.CostEstimate(flops=1 << 21, bytes_accessed=1 << 22, transcendentals=0),
        name="turn_tokens",
    )(place, near)


def hidden_kernel(group_ref, side_ref, rows_ref, out_ref):
    product, square = 0.0, 0.0
    for t in range(side_ref.shape[0]):
        side = side_ref[t]
        product = product + jnp.dot(
            side, rows_ref[:, t].reshape(512, WIDTH), preferred_element_type=f32
        )
        wide = side.astype(f32)
        terms = wide * wide
        for k in range(4):
            square = square + terms[:, k * 128 : (k + 1) * 128]

    @pl.when(pl.program_id(0) == 0)
    def _():
        out_ref[:, :WIDTH] = product
        out_ref[:, WIDTH:] = square

    @pl.when(pl.program_id(0) > 0)
    def _():
        out_ref[:, :WIDTH] += product
        out_ref[:, WIDTH:] += square


def partial_hidden(group, side, rows):
    return pl.pallas_call(
        hidden_kernel,
        grid_spec=pltpu.PrefetchScalarGridSpec(
            num_scalar_prefetch=1,
            grid=(2,),
            in_specs=[
                pl.BlockSpec((2, TOKENS, 512), lambda t, group: (t, group[0], 0)),
                pl.BlockSpec((8, 2, 64, WIDTH), lambda t, group: (0, t, 0, 0)),
            ],
            out_specs=pl.BlockSpec((TOKENS, 1024), lambda t, group: (0, 0)),
        ),
        out_shape=jax.ShapeDtypeStruct((TOKENS, 1024), f32),
        cost_estimate=pl.CostEstimate(
            flops=2 * TOKENS * 2048 * WIDTH, bytes_accessed=6 << 20, transcendentals=0
        ),
        compiler_params=pltpu.CompilerParams(vmem_limit_bytes=24 << 20),
        name="partial_hidden",
    )(group, side, pltpu.with_memory_space_constraint(rows, pltpu.HBM))


def label_kernel(own_ref, other_ref, pair_ref, head_ref, out_ref):
    both = own_ref[...] + other_ref[...]
    mean = jnp.sum(both[:, WIDTH:], axis=1, keepdims=True) / 4096.0
    hidden = both[:, :WIDTH] * lax.rsqrt(mean + 1e-05)
    active = hidden / (1.0 + jnp.exp(-hidden))
    pairs = lax.broadcasted_iota(jnp.int32, (PAIRS, TOKENS), 0)
    member = jnp.where(pair_ref[...] == pairs, 1.0, 0.0)
    hot = member.astype(bf16)
    dot = functools.partial(jnp.dot, preferred_element_type=f32)
    first = active.astype(bf16)
    rest = active - first.astype(f32)
    second = rest.astype(bf16)
    third = (rest - second.astype(f32)).astype(bf16)
    totals = dot(hot, first) + (dot(hot, second) + dot(hot, third))
    pooled = (totals / jnp.sum(member, axis=1, keepdims=True)).astype(bf16)
    out_ref[...] = dot(pooled, head_ref[...])


def label_pairs(own, other, pairs, head):
    return pl.pallas_call(
        label_kernel,
        out_shape=jax.ShapeDtypeStruct((PAIRS, 256), f32),
        in_specs=[pl.BlockSpec(memory_space=VMEM)] * 4,
        out_specs=pl.BlockSpec(memory_space=VMEM),
        cost_estimate=pl.CostEstimate(
            flops=2 * 32 * TOKENS * WIDTH, bytes_accessed=3 << 20, transcendentals=TOKENS * WIDTH
        ),
        compiler_params=pltpu.CompilerParams(vmem_limit_bytes=16 << 20),
        name="label_pairs",
    )(own, other, pairs, head)


def shards(
    master_weight,
    first_moment,
    second_moment,
    teacher_weight,
    grad_parts,
    embed_table,
    token_ids,
    pair_ids,
    class_head,
):
    every_id = lax.all_to_all(
        jnp.broadcast_to(token_ids[None], (32, 1, TOKENS)), ("z", "yl", "c"), 0, 0, tiled=True
    )
    gradient = lax.psum_scatter(grad_parts[0], "dp", scatter_dimension=0, tiled=True)
    table = turn_table(embed_table)
    picked = pick_tokens(every_id, table)
    received = lax.all_to_all(
        picked, ("z", "yl"), 0, 0, tiled=True
    )
    state = (
        master_weight, first_moment, second_moment, teacher_weight,
        pltpu.with_memory_space_constraint(gradient, pltpu.HBM),
    )
    columns = teacher_columns(*state)
    master_new, first_new, second_new, teacher_new = optimizer_step(*state)
    block = lax.all_to_all(columns.reshape(8, 32, WIDTH), ("yl", "dp"), 0, 0, tiled=True)
    sorted_block = block.reshape(8, 4, 8, WIDTH).transpose(1, 0, 2, 3).reshape(256, WIDTH)
    rows = lax.all_gather(sorted_block, "z", axis=0, tiled=True)
    parts = [received]
    for k in (1, 3, 2):
        parts.append(lax.ppermute(received, "dp", [(i, i ^ k) for i in range(4)]))
    near = jnp.stack([parts[0], parts[1], parts[3], parts[2]])
    place = lax.axis_index("dp").astype(jnp.int32).reshape(1)
    turned = turn_tokens(place, near)
    side = lax.all_to_all(turned, "t", 0, 0, tiled=True)
    rows = rows.reshape(8, 4, 64, WIDTH)
    core = lax.axis_index("c").astype(jnp.int32).reshape(1)
    sent = partial_hidden(1 - core, side, rows)
    other = lax.ppermute(sent, "c", [(0, 1), (1, 0)])
    own = partial_hidden(core, side, rows)
    terms = label_pairs(own, other, pair_ids, class_head[0])
    every_term = lax.all_to_all(
        jnp.broadcast_to(terms[None], (16, PAIRS, 256)), ("dp", "t"), 0, 0, tiled=True
    )
    class_logits = jnp.sum(every_term, axis=0, keepdims=True)
    return (master_new, first_new, second_new, teacher_new, class_logits)


def solution(mesh):
    fine = Mesh(mesh.devices.reshape(8, 2, 2, 4, 4), ("z", "yl", "c", "dp", "t"))
    fsdp = ("z", "yl", "c")
    rows = P(fsdp + ("dp",), "t")
    return jax.shard_map(
        shards,
        mesh=fine,
        in_specs=(
            rows,
            rows,
            rows,
            rows,
            P("dp", fsdp, "t"),
            P(fsdp + ("dp", "t"), None),
            P(fsdp, None),
            P(fsdp, None),
            P("t", "dp", None),
        ),
        out_specs=(rows, rows, rows, rows, P(fsdp, None, None)),
        check_vma=False,
    )
```
